128 devices in a mesh: dp: 4 (over z), expert: 32 (over x, y, core).
Axes of the slice: x: 4, y: 4, z: 4, core: 2. Of those that a mesh axis runs over, the one named last changes fastest.
Arguments:
- grad_parts: bfloat16 [4, 128, 128, 2048], P('dp', 'expert'), may hold values from -6 to 6
- first_moment: float32 [128, 128, 2048], P('expert', None, 'dp'), may hold values from -4 to 4
- second_moment: float32 [128, 128, 2048], P('expert', None, 'dp'), may hold values from 0.05 to 2
- master_weight: float32 [128, 128, 2048], P('expert', None, 'dp'), may hold values from -6 to 6
- old_owner: int32 [104], replicated, may hold values from 0 to 25, as said below
- new_owner: int32 [104], replicated, may hold values from 0 to 31, as said below
Outputs:
- new_master: float32 [192, 128, 2048], P('expert', None, 'dp')
- new_first: float32 [192, 128, 2048], P('expert', None, 'dp')
- new_second: float32 [192, 128, 2048], P('expert', None, 'dp')
- new_params: bfloat16 [192, 128, 2048], P('expert')
The draws below stay inside these ranges and needn't reach their ends.
Inputs may be any that keep to these rules, and one draw needn't show every extreme that they name: `old_owner`: tiles are owned by devices 0 to 25 of the expert axis, exactly 4 each; the other devices own none, and their slots of the old-layout arrays are never read. `new_owner`: each device owns at most 6 tiles and some own exactly 6; the tiles of one old owner go to different new owners.
All inputs are finite; a program needn't handle non-finite values.
Results may differ from the reference program's by a relative error of at most 0.0085.
Values may be sent and summed in bfloat16 or wider, within the bound.
No kernel may reach another device: no remote copies, remote signals or barrier semaphores. Data moves between devices by JAX's collectives and lax.ppermute only.
A program may use at most 128 MiB of HBM per device.

```python
import math
import jax
import jax.numpy as jnp
from jax import lax

FF = 2048
TILE_ROWS = 128
OLD_SLOTS = 4
OLD_DEV = 26
NEW_SLOTS = 6
HOT = 4
TILES = 104
N_DP = 4
N_EXPERT = 32


def owner_maps(key):
    key_perm, key_place = jax.random.split(jax.random.fold_in(key, 7))
    shuffle = jax.random.permutation(key_perm, TILES).astype(jnp.int32)
    counter = jnp.arange(TILES, dtype=jnp.int32)
    old_map = jnp.zeros((TILES,), jnp.int32).at[shuffle].set(counter // OLD_SLOTS)
    device_ids = jnp.arange(N_EXPERT, dtype=jnp.int32)
    remaining = TILES - HOT * NEW_SLOTS
    base_load = remaining // (N_EXPERT - HOT)
    extra_load = remaining % (N_EXPERT - HOT)
    load_sizes = jnp.where(device_ids < HOT, NEW_SLOTS, base_load + (device_ids - HOT < extra_load).astype(jnp.int32))
    bounds = jnp.cumsum(load_sizes).astype(jnp.int32)
    position = jnp.sum((counter[:, None] >= bounds[None, :]).astype(jnp.int32), axis=1)
    slot_part = counter // OLD_DEV
    owner_part = counter % OLD_DEV
    tile_ids = shuffle[owner_part * OLD_SLOTS + slot_part]
    relabel = jax.random.permutation(key_place, N_EXPERT).astype(jnp.int32)
    new_map = jnp.zeros((TILES,), jnp.int32).at[tile_ids].set(relabel[position])
    return (old_map, new_map)


def draw_old_owner(key, part):
    return owner_maps(key)[0]


def draw_new_owner(key, part):
    return owner_maps(key)[1]


def block_scale(own_key, dims, shards, least, high):
    gain = 1.0
    for axis_at, shards_of in shards:
        draws = jax.random.uniform(jax.random.fold_in(jax.random.fold_in(own_key, 6), axis_at), (shards_of,), jnp.float32, least / len(shards), high / len(shards))
        gain = gain * jnp.repeat(jnp.exp(draws), dims[axis_at] // shards_of).reshape((-1,) + (1,) * (len(dims) - 1 - axis_at))
    return gain


def noise(key, dims, width, reach, cuts=(), kind=jnp.bfloat16):
    array = jax.random.normal(key, dims, jnp.float32) * width
    if len(cuts) > 0:
        array = block_scale(key, dims, cuts, -0.22, 0.18) * array
    return jnp.clip(array, min=-reach, max=reach).astype(kind)


def setup_inputs(seed: int = 0) -> dict:
    keys = jax.random.split(jax.random.key(seed), 7)
    return {
        "grad_parts": noise(keys[0], (N_DP, N_EXPERT * OLD_SLOTS, TILE_ROWS, FF), 1.0, 6.0, ((0, 4), (1, 32))),
        "first_moment": noise(keys[1], (N_EXPERT * OLD_SLOTS, TILE_ROWS, FF), 0.3, 4.0, ((0, 32), (2, 4)), jnp.float32),
        "second_moment": jnp.clip(jnp.exp(math.log(2.0) - 3.6888794 * jax.random.uniform(keys[2], (N_EXPERT * OLD_SLOTS, TILE_ROWS, FF), jnp.float32) ** block_scale(keys[2], (N_EXPERT * OLD_SLOTS, TILE_ROWS, FF), ((0, 32), (2, 4)), -0.2, 0.2)), 0.05, 2.0),
        "master_weight": noise(keys[3], (N_EXPERT * OLD_SLOTS, TILE_ROWS, FF), 0.5, 6.0, ((0, 32), (2, 4)), jnp.float32),
        "old_owner": draw_old_owner(jax.random.fold_in(keys[6], 71), 0),
        "new_owner": draw_new_owner(jax.random.fold_in(keys[6], 71), 0),
    }


def slot_ranks(owner, count):
    matches = (owner[:, None] == jnp.arange(count, dtype=jnp.int32)[None, :]).astype(jnp.int32)
    before = jnp.cumsum(matches, axis=0) - matches
    return lax.optimization_barrier(jnp.sum(before * matches, axis=1)).astype(jnp.int32)

def adam_step(gradient, moment_one, moment_two, weight):
    moment_one = 0.9 * moment_one + 0.1 * gradient
    moment_two = 0.95 * moment_two + 0.05 * gradient * gradient
    update = moment_one / (1.0 - 0.9 ** 50) / (jnp.sqrt(moment_two / (1.0 - 0.95 ** 50)) + 1e-08)
    weight = weight - 0.05 * (update + 0.1 * weight)
    return (weight, moment_one, moment_two)

def reference(grad_parts, first_moment, second_moment, master_weight, old_owner, new_owner):
    old_rank = slot_ranks(old_owner, N_EXPERT)
    new_rank = slot_ranks(new_owner, N_EXPERT)
    source_rows = (old_owner * OLD_SLOTS + old_rank).astype(jnp.int32)
    target_rows = (new_owner * NEW_SLOTS + new_rank).astype(jnp.int32)
    gradient = jnp.zeros((TILES, TILE_ROWS, FF), jnp.float32)
    for replica in range(N_DP):
        gradient = gradient + grad_parts[replica][source_rows].astype(jnp.float32)
    weight, moment_one, moment_two = adam_step(gradient, first_moment[source_rows], second_moment[source_rows], master_weight[source_rows])
    empty = jnp.zeros((N_EXPERT * NEW_SLOTS, TILE_ROWS, FF), jnp.float32)
    new_master = empty.at[target_rows].set(weight)
    new_first = empty.at[target_rows].set(moment_one)
    new_second = empty.at[target_rows].set(moment_two)
    return (new_master, new_first, new_second, new_master.astype(jnp.bfloat16))
```

```python
import jax
import jax.numpy as jnp
from jax import lax
from jax.experimental import pallas as pl
from jax.experimental.pallas import tpu as pltpu
from jax.sharding import PartitionSpec as P

BF16 = jnp.bfloat16
F32 = jnp.float32
PEERS = 32
OLD = 4
NEW = 6
PR, PC = 8, 256
STEPS = 4


def route_kernel(old_ref, new_ref, table_ref, old_count, new_count):
    def clear_counts(i, _):
        old_count[i] = 0
        new_count[i] = 0
        return 0

    def clear_table(i, _):
        table_ref[i] = -1
        return 0

    lax.fori_loop(0, PEERS, clear_counts, 0)
    lax.fori_loop(0, PEERS * NEW, clear_table, 0)

    def place(t, _):
        o = old_ref[t]
        n = new_ref[t]
        a = old_count[o]
        b = new_count[n]
        table_ref[n * NEW + b] = o * OLD + a
        old_count[o] = a + 1
        new_count[n] = b + 1
        return 0

    lax.fori_loop(0, old_ref.shape[0], place, 0)


def route(old_owner, new_owner):
    smem = pl.BlockSpec(memory_space=pltpu.SMEM)
    return pl.pallas_call(
        route_kernel,
        out_shape=jax.ShapeDtypeStruct((PEERS * NEW,), jnp.int32),
        in_specs=[smem, smem],
        out_specs=smem,
        scratch_shapes=[pltpu.SMEM((PEERS,), jnp.int32), pltpu.SMEM((PEERS,), jnp.int32)],
        name="route",
    )(old_owner, new_owner)


def pack_state_kernel(m1_ref, m2_ref, w_ref, out_ref):
    for k, ref in enumerate((m1_ref, m2_ref, w_ref)):
        for r in range(ref.shape[1] // PR):
            for c in range(2):
                piece = ref[:, r * PR : (r + 1) * PR, c * PC : (c + 1) * PC]
                out_ref[2 * r + c, :, k] = piece.astype(BF16)


def pack_state(m1, m2, w):
    rows = 128 // STEPS
    block = pl.BlockSpec((OLD, rows, 512), lambda i: (0, i, 0))
    return pl.pallas_call(
        pack_state_kernel,
        grid=(STEPS,),
        out_shape=jax.ShapeDtypeStruct((PEERS, OLD, 3, PR, PC), BF16),
        in_specs=[block] * 3,
        out_specs=pl.BlockSpec((PEERS // STEPS, OLD, 3, PR, PC), lambda i: (i, 0, 0, 0, 0)),
        name="pack_state",
    )(m1, m2, w)


def pack_grad_kernel(g_ref, out_ref):
    for r in range(g_ref.shape[1] // PR):
        for c in range(2):
            out_ref[2 * r + c] = g_ref[:, r * PR : (r + 1) * PR, c * PC : (c + 1) * PC]


def pack_grad(g):
    return pl.pallas_call(
        pack_grad_kernel,
        out_shape=jax.ShapeDtypeStruct((PEERS, OLD, PR, PC), BF16),
        name="pack_grad",
    )(g)


def adam_step(gradient, moment_one, moment_two, weight):
    moment_one = 0.9 * moment_one + 0.1 * gradient
    moment_two = 0.95 * moment_two + 0.05 * gradient * gradient
    update = moment_one / (1.0 - 0.9**50) / (jnp.sqrt(moment_two / (1.0 - 0.95**50)) + 1e-08)
    weight = weight - 0.05 * (update + 0.1 * weight)
    return (weight, moment_one, moment_two)


def update_kernel(table_ref, state_ref, grad_ref, weight_ref, moments_ref):
    def owner(d, _):
        for s in range(NEW):
            row = table_ref[d * NEW + s]
            has = row >= 0
            row = jnp.maximum(row, 0)
            gradient = grad_ref[row].astype(F32)
            m1 = state_ref[row, 0].astype(F32)
            m2 = state_ref[row, 1].astype(F32)
            w = state_ref[row, 2].astype(F32)
            w, m1, m2 = adam_step(gradient, m1, m2, w)
            weight_ref[d, s] = jnp.where(has, w, 0.0).astype(BF16)
            moments_ref[d, s, 0] = jnp.where(has, m1, 0.0).astype(BF16)
            moments_ref[d, s, 1] = jnp.where(has, m2, 0.0).astype(BF16)
        return 0

    lax.fori_loop(0, PEERS, owner, 0)


def update(table, state, grad):
    vmem = pl.BlockSpec(memory_space=pltpu.VMEM)
    return pl.pallas_call(
        update_kernel,
        out_shape=(
            jax.ShapeDtypeStruct((PEERS, NEW, PR, PC), BF16),
            jax.ShapeDtypeStruct((PEERS, NEW, 2, PR, PC), BF16),
        ),
        in_specs=[pl.BlockSpec(memory_space=pltpu.SMEM), vmem, vmem],
        out_specs=(vmem, vmem),
        compiler_params=pltpu.CompilerParams(vmem_limit_bytes=32 * 1024 * 1024),
        name="update",
    )(table, state, grad)


def unpack_state_kernel(w_ref, m_ref, w_out, m1_out, m2_out):
    for r in range(w_out.shape[1] // PR):
        for c in range(2):
            at = (slice(None), slice(r * PR, (r + 1) * PR), slice(c * PC, (c + 1) * PC))
            w_out[at] = w_ref[2 * r + c].astype(F32)
            m1_out[at] = m_ref[2 * r + c, :, 0].astype(F32)
            m2_out[at] = m_ref[2 * r + c, :, 1].astype(F32)


def unpack_state(w, m):
    rows = 128 // STEPS
    out = jax.ShapeDtypeStruct((NEW, 128, 512), F32)
    return pl.pallas_call(
        unpack_state_kernel,
        grid=(STEPS,),
        out_shape=(out, out, out),
        in_specs=[
            pl.BlockSpec((PEERS // STEPS, NEW, PR, PC), lambda i: (i, 0, 0, 0)),
            pl.BlockSpec((PEERS // STEPS, NEW, 2, PR, PC), lambda i: (i, 0, 0, 0, 0)),
        ],
        out_specs=[pl.BlockSpec((NEW, rows, 512), lambda i: (0, i, 0))] * 3,
        name="unpack_state",
    )(w, m)


def unpack_params_kernel(w_ref, out_ref):
    for z in range(w_ref.shape[0]):
        for r in range(out_ref.shape[1] // PR):
            for c in range(2):
                lanes = slice(z * 512 + c * PC, z * 512 + (c + 1) * PC)
                out_ref[:, r * PR : (r + 1) * PR, lanes] = w_ref[z, 2 * r + c]


def unpack_params(w):
    rows = 128 // STEPS
    n = w.shape[0]
    return pl.pallas_call(
        unpack_params_kernel,
        grid=(STEPS,),
        out_shape=jax.ShapeDtypeStruct((NEW, 128, 512 * n), BF16),
        in_specs=[pl.BlockSpec((n, PEERS // STEPS, NEW, PR, PC), lambda i: (0, i, 0, 0, 0))],
        out_specs=pl.BlockSpec((NEW, rows, 512 * n), lambda i: (0, i, 0)),
        name="unpack_params",
    )(w)


def exchange(values):
    return lax.all_to_all(values, "expert", split_axis=0, concat_axis=0, tiled=True)


def shards(grad_parts, first_moment, second_moment, master_weight, old_owner, new_owner):
    summed = lax.psum_scatter(grad_parts[0], "dp", scatter_dimension=2, tiled=True)
    table = route(old_owner, new_owner)
    state = exchange(pack_state(first_moment, second_moment, master_weight))
    grad = exchange(pack_grad(summed))
    weight, moments = update(
        table,
        state.reshape(PEERS * OLD, 3, PR, PC),
        grad.reshape(PEERS * OLD, PR, PC),
    )
    weight = exchange(weight)
    weight, moments = lax.optimization_barrier((weight, moments))
    moments = exchange(moments)
    gathered = lax.all_gather(weight, "dp", axis=0, tiled=False)
    new_master, new_first, new_second = unpack_state(weight, moments)
    new_params = unpack_params(gathered)
    return (new_master, new_first, new_second, new_params)


def solution(mesh):
    placed = (
        P("dp", "expert", None, None),
        P("expert", None, "dp"),
        P("expert", None, "dp"),
        P("expert", None, "dp"),
        P(),
        P(),
    )
    return jax.shard_map(
        shards,
        mesh=mesh,
        in_specs=placed,
        out_specs=(
            P("expert", None, "dp"),
            P("expert", None, "dp"),
            P("expert", None, "dp"),
            P("expert", None, None),
        ),
        check_vma=False,
    )
```

```python
import functools

import jax
import jax.numpy as jnp
from jax import lax
from jax.experimental import pallas as pl
from jax.experimental.pallas import tpu as pltpu
from jax.sharding import PartitionSpec as P

BF16 = jnp.bfloat16
F32 = jnp.float32
PEERS = 32
OLD = 4
NEW = 6
PR, PC = 8, 256
STEPS = 4
VMEM = pl.BlockSpec(memory_space=pltpu.VMEM)


def route_kernel(old_ref, new_ref, table_ref, old_count, new_count):
    def clear_counts(i, _):
        old_count[i] = 0
        new_count[i] = 0
        return 0

    def clear_table(i, _):
        table_ref[i] = -1
        return 0

    lax.fori_loop(0, PEERS, clear_counts, 0)
    lax.fori_loop(0, PEERS * NEW, clear_table, 0)

    def place(t, _):
        o = old_ref[t]
        n = new_ref[t]
        a = old_count[o]
        b = new_count[n]
        table_ref[n * NEW + b] = o * OLD + a
        old_count[o] = a + 1
        new_count[n] = b + 1
        return 0

    lax.fori_loop(0, old_ref.shape[0], place, 0)


def route(old_owner, new_owner):
    smem = pl.BlockSpec(memory_space=pltpu.SMEM)
    return pl.pallas_call(
        route_kernel,
        out_shape=jax.ShapeDtypeStruct((PEERS * NEW,), jnp.int32),
        in_specs=[smem, smem],
        out_specs=smem,
        scratch_shapes=[pltpu.SMEM((PEERS,), jnp.int32), pltpu.SMEM((PEERS,), jnp.int32)],
        name="route",
    )(old_owner, new_owner)


def pack_state_kernel(m1_ref, m2_ref, w_ref, out_ref):
    for k, ref in enumerate((m1_ref, m2_ref, w_ref)):
        for r in range(ref.shape[1] // PR):
            for c in range(2):
                piece = ref[:, r * PR : (r + 1) * PR, c * PC : (c + 1) * PC]
                out_ref[2 * r + c, :, k] = piece.astype(BF16)


def pack_state(m1, m2, w):
    rows = 128 // STEPS
    block = pl.BlockSpec((OLD, rows, 512), lambda i: (0, i, 0))
    return pl.pallas_call(
        pack_state_kernel,
        grid=(STEPS,),
        out_shape=jax.ShapeDtypeStruct((PEERS, OLD, 3, PR, PC), BF16),
        in_specs=[block] * 3,
        out_specs=pl.BlockSpec((PEERS // STEPS, OLD, 3, PR, PC), lambda i: (i, 0, 0, 0, 0)),
        name="pack_state",
    )(m1, m2, w)


def pack_halves_kernel(ahead, me_ref, *refs):
    del me_ref
    for g_ref, a_ref, b_ref in zip(refs[:ahead], refs[ahead::2], refs[ahead + 1 :: 2]):
        for r in range(g_ref.shape[2] // PR):
            for c in range(2):
                rows, lanes = slice(r * PR, (r + 1) * PR), slice(c * PC, (c + 1) * PC)
                a_ref[2 * r + c] = g_ref[:, 0, rows, lanes]
                b_ref[2 * r + c] = g_ref[:, 1, rows, lanes]


def shard_block(steps, ahead):
    return pl.BlockSpec((OLD, 2, 64 // steps, 512), lambda i, me: (0, 0, i, (me[0] + ahead) % 4))


def half_block(steps, slots):
    return pl.BlockSpec((PEERS // 2 // steps, slots, PR, PC), lambda i, me: (i, 0, 0, 0))


def pack_halves(me, g, aheads, name):
    steps = 2
    n = len(aheads)
    half = jax.ShapeDtypeStruct((PEERS // 2, OLD, PR, PC), BF16)
    return pl.pallas_call(
        functools.partial(pack_halves_kernel, n),
        grid_spec=pltpu.PrefetchScalarGridSpec(
            num_scalar_prefetch=1,
            grid=(steps,),
            in_specs=[shard_block(steps, k) for k in aheads],
            out_specs=[half_block(steps, OLD)] * (2 * n),
        ),
        out_shape=[half] * (2 * n),
        name=name,
    )(me, *([g] * n))


def sum_grad_kernel(own_a, own_b, ua, ub, da, db, out_ref):
    half = PEERS // 2
    for h, refs in enumerate(((own_a, ua, da), (own_b, ub, db))):
        for j in range(half):
            own, up, down = (ref[j].astype(F32) for ref in refs)
            out_ref[h * half + j] = (own + up + down).astype(BF16)


def sum_grad(*halves):
    return pl.pallas_call(
        sum_grad_kernel,
        out_shape=jax.ShapeDtypeStruct((PEERS, OLD, PR, PC), BF16),
        in_specs=[VMEM] * 6,
        out_specs=VMEM,
        name="sum_grad",
    )(*halves)


def adam_step(gradient, moment_one, moment_two, weight):
    moment_one = 0.9 * moment_one + 0.1 * gradient
    moment_two = 0.95 * moment_two + 0.05 * gradient * gradient
    update = moment_one / (1.0 - 0.9**50) / (jnp.sqrt(moment_two / (1.0 - 0.95**50)) + 1e-08)
    weight = weight - 0.05 * (update + 0.1 * weight)
    return (weight, moment_one, moment_two)


def update_kernel(table_ref, state_ref, grad_ref, weight_ref, moments_ref):
    def owner(d, _):
        for s in range(NEW):
            row = table_ref[d * NEW + s]
            has = row >= 0
            row = jnp.maximum(row, 0)
            gradient = grad_ref[row].astype(F32)
            m1 = state_ref[row, 0].astype(F32)
            m2 = state_ref[row, 1].astype(F32)
            w = state_ref[row, 2].astype(F32)
            w, m1, m2 = adam_step(gradient, m1, m2, w)
            weight_ref[d, s] = jnp.where(has, w, 0.0).astype(BF16)
            moments_ref[d, s, 0] = jnp.where(has, m1, 0.0).astype(BF16)
            moments_ref[d, s, 1] = jnp.where(has, m2, 0.0).astype(BF16)
        return 0

    lax.fori_loop(0, PEERS, owner, 0)


def update(table, state, grad):
    vmem = pl.BlockSpec(memory_space=pltpu.VMEM)
    return pl.pallas_call(
        update_kernel,
        out_shape=(
            jax.ShapeDtypeStruct((PEERS, NEW, PR, PC), BF16),
            jax.ShapeDtypeStruct((PEERS, NEW, 2, PR, PC), BF16),
        ),
        in_specs=[pl.BlockSpec(memory_space=pltpu.SMEM), vmem, vmem],
        out_specs=(vmem, vmem),
        compiler_params=pltpu.CompilerParams(vmem_limit_bytes=32 * 1024 * 1024),
        name="update",
    )(table, state, grad)


def unpack_own_kernel(me_ref, w_ref, w_out, out_ref):
    del me_ref
    n = w_out.shape[1] // PR
    for r in range(n):
        for c in range(2):
            rows, lanes = slice(r * PR, (r + 1) * PR), slice(c * PC, (c + 1) * PC)
            piece = w_ref[2 * r + c]
            w_out[:, rows, lanes] = piece.astype(F32)
            out_ref[:, rows, lanes] = piece


def unpack_own(me, w):
    rows = 128 // STEPS
    return pl.pallas_call(
        unpack_own_kernel,
        grid_spec=pltpu.PrefetchScalarGridSpec(
            num_scalar_prefetch=1,
            grid=(STEPS,),
            in_specs=[pl.BlockSpec((PEERS // STEPS, NEW, PR, PC), lambda i, me: (i, 0, 0, 0))],
            out_specs=[
                pl.BlockSpec((NEW, rows, 512), lambda i, me: (0, i, 0)),
                pl.BlockSpec((NEW, rows, 512), lambda i, me: (0, i, me[0])),
            ],
        ),
        out_shape=(
            jax.ShapeDtypeStruct((NEW, 128, 512), F32),
            jax.ShapeDtypeStruct((NEW, 128, 2048), BF16),
        ),
        name="unpack_own",
    )(me, w)


def unpack_moments_kernel(m_ref, m1_out, m2_out):
    for r in range(m1_out.shape[1] // PR):
        for c in range(2):
            rows, lanes = slice(r * PR, (r + 1) * PR), slice(c * PC, (c + 1) * PC)
            m1_out[:, rows, lanes] = m_ref[2 * r + c, :, 0].astype(F32)
            m2_out[:, rows, lanes] = m_ref[2 * r + c, :, 1].astype(F32)


def unpack_moments(m):
    rows = 128 // STEPS
    out = jax.ShapeDtypeStruct((NEW, 128, 512), F32)
    return pl.pallas_call(
        unpack_moments_kernel,
        grid=(STEPS,),
        out_shape=(out, out),
        in_specs=[pl.BlockSpec((PEERS // STEPS, NEW, 2, PR, PC), lambda i: (i, 0, 0, 0, 0))],
        out_specs=[pl.BlockSpec((NEW, rows, 512), lambda i: (0, i, 0))] * 2,
        name="unpack_moments",
    )(m)


def unpack_block_kernel(me_ref, a_ref, b_ref, old_ref, out_ref):
    del me_ref, old_ref
    for r in range(out_ref.shape[2] // PR):
        for c in range(2):
            rows, lanes = slice(r * PR, (r + 1) * PR), slice(c * PC, (c + 1) * PC)
            out_ref[:, 0, rows, lanes] = a_ref[2 * r + c]
            out_ref[:, 1, rows, lanes] = b_ref[2 * r + c]


def unpack_block(me, a, b, params, ahead):
    steps = 2
    return pl.pallas_call(
        unpack_block_kernel,
        grid_spec=pltpu.PrefetchScalarGridSpec(
            num_scalar_prefetch=1,
            grid=(steps,),
            in_specs=[half_block(steps, NEW)] * 2 + [pl.BlockSpec(memory_space=pl.ANY)],
            out_specs=pl.BlockSpec((NEW, 2, 64 // steps, 512), lambda i, me: (0, 0, i, (me[0] + ahead) % 4)),
        ),
        out_shape=jax.ShapeDtypeStruct((NEW, 2, 64, 2048), BF16),
        input_output_aliases={3: 0},
        name="unpack_block",
    )(me, a, b, params)


UP = [(i, (i + 1) % 4) for i in range(4)]
DOWN = [(i, (i - 1) % 4) for i in range(4)]


def send_up(x):
    return lax.ppermute(x, "dp", UP)


def send_down(x):
    return lax.ppermute(x, "dp", DOWN)


def add(x, y):
    return (x.astype(F32) + y.astype(F32)).astype(BF16)


def exchange(values):
    return lax.all_to_all(values, "expert", split_axis=0, concat_axis=0, tiled=True)


def shards(grad_parts, first_moment, second_moment, master_weight, old_owner, new_owner):
    me = lax.axis_index("dp").astype(jnp.int32)[None]
    g = grad_parts[0].reshape(OLD, 2, 64, 2048)
    far_a, far_b = pack_halves(me, g, (2,), "pack_far")
    far_up, far_down = send_up(far_a), send_down(far_b)
    state = pack_state(first_moment, second_moment, master_weight)
    state, g = lax.optimization_barrier((state, g))
    state = exchange(state)
    up_a, up_b, down_a, down_b, own_a, own_b = pack_halves(me, g, (1, 3, 0), "pack_near")
    ub, da = send_up(up_b), send_down(down_a)
    ua, db = send_up(add(up_a, far_up)), send_down(add(down_b, far_down))
    state, ua, ub, da, db = lax.optimization_barrier((state, ua, ub, da, db))
    grad = exchange(sum_grad(own_a, own_b, ua, ub, da, db))
    table = route(old_owner, new_owner)
    weight, moments = update(
        table,
        state.reshape(PEERS * OLD, 3, PR, PC),
        grad.reshape(PEERS * OLD, PR, PC),
    )
    weight = exchange(weight)
    weight, moments = lax.optimization_barrier((weight, moments))
    wa, wb = weight[: PEERS // 2], weight[PEERS // 2 :]
    ua, da = send_up(wa), send_down(wa)
    ub, db = send_up(wb), send_down(wb)
    fa, fb = send_up(ua), send_down(db)
    moments = exchange(moments)
    new_master, params = unpack_own(me, weight)
    params = params.reshape(NEW, 2, 64, 2048)
    params = unpack_block(me, ua, ub, params, 3)
    params = unpack_block(me, da, db, params, 1)
    new_first, new_second = unpack_moments(moments)
    fa, fb, new_first = lax.optimization_barrier((fa, fb, new_first))
    new_params = unpack_block(me, fa, fb, params, 2).reshape(NEW, 128, 2048)
    return (new_master, new_first, new_second, new_params)


def solution(mesh):
    placed = (
        P("dp", "expert", None, None),
        P("expert", None, "dp"),
        P("expert", None, "dp"),
        P("expert", None, "dp"),
        P(),
        P(),
    )
    return jax.shard_map(
        shards,
        mesh=mesh,
        in_specs=placed,
        out_specs=(
            P("expert", None, "dp"),
            P("expert", None, "dp"),
            P("expert", None, "dp"),
            P("expert", None, None),
        ),
        check_vma=False,
    )
```

```python
import functools

import jax
import jax.numpy as jnp
from jax import lax
from jax.experimental import pallas as pl
from jax.experimental.pallas import tpu as pltpu
from jax.sharding import PartitionSpec as P

BF16 = jnp.bfloat16
F32 = jnp.float32
PEERS = 32
OLD = 4
NEW = 6
PR, PC = 8, 256
STEPS = 2
PARAMS = pltpu.CompilerParams(vmem_limit_bytes=16 * 1024 * 1024)
VMEM = pl.BlockSpec(memory_space=pltpu.VMEM)


def route_kernel(old_ref, new_ref, table_ref, old_count, new_count):
    def clear_counts(i, _):
        old_count[i] = 0
        new_count[i] = 0
        return 0

    def clear_table(i, _):
        table_ref[i] = -1
        return 0

    lax.fori_loop(0, PEERS, clear_counts, 0)
    lax.fori_loop(0, PEERS * NEW, clear_table, 0)

    def place(t, _):
        o = old_ref[t]
        n = new_ref[t]
        a = old_count[o]
        b = new_count[n]
        table_ref[n * NEW + b] = o * OLD + a
        old_count[o] = a + 1
        new_count[n] = b + 1
        return 0

    lax.fori_loop(0, old_ref.shape[0], place, 0)


def route(old_owner, new_owner):
    smem = pl.BlockSpec(memory_space=pltpu.SMEM)
    return pl.pallas_call(
        route_kernel,
        out_shape=jax.ShapeDtypeStruct((PEERS * NEW,), jnp.int32),
        in_specs=[smem, smem],
        out_specs=smem,
        scratch_shapes=[pltpu.SMEM((PEERS,), jnp.int32), pltpu.SMEM((PEERS,), jnp.int32)],
        compiler_params=PARAMS,
        name="route",
    )(old_owner, new_owner)


def pack_state_kernel(m1_ref, m2_ref, w_ref, out_ref):
    for k, ref in enumerate((m1_ref, m2_ref, w_ref)):
        for r in range(ref.shape[1] // PR):
            for c in range(2):
                piece = ref[:, r * PR : (r + 1) * PR, c * PC : (c + 1) * PC]
                out_ref[2 * r + c, :, k] = piece.astype(BF16)


def pack_state(m1, m2, w):
    rows = 128 // STEPS
    block = pl.BlockSpec((OLD, rows, 512), lambda i: (0, i, 0))
    return pl.pallas_call(
        pack_state_kernel,
        grid=(STEPS,),
        out_shape=jax.ShapeDtypeStruct((PEERS, OLD, 3, PR, PC), BF16),
        in_specs=[block] * 3,
        out_specs=pl.BlockSpec((PEERS // STEPS, OLD, 3, PR, PC), lambda i: (i, 0, 0, 0, 0)),
        name="pack_state",
    )(m1, m2, w)


def pack_halves_kernel(ahead, me_ref, *refs):
    del me_ref
    for g_ref, a_ref, b_ref in zip(refs[:ahead], refs[ahead::2], refs[ahead + 1 :: 2]):
        for r in range(g_ref.shape[2] // PR):
            for c in range(2):
                rows, lanes = slice(r * PR, (r + 1) * PR), slice(c * PC, (c + 1) * PC)
                a_ref[2 * r + c] = g_ref[:, 0, rows, lanes]
                b_ref[2 * r + c] = g_ref[:, 1, rows, lanes]


def shard_block(steps, ahead):
    return pl.BlockSpec((OLD, 2, 64 // steps, 512), lambda i, me: (0, 0, i, (me[0] + ahead) % 4))


def half_block(steps, slots):
    return pl.BlockSpec((PEERS // 2 // steps, slots, PR, PC), lambda i, me: (i, 0, 0, 0))


def pack_halves(me, g, aheads, name):
    steps = 2
    n = len(aheads)
    half = jax.ShapeDtypeStruct((PEERS // 2, OLD, PR, PC), BF16)
    return pl.pallas_call(
        functools.partial(pack_halves_kernel, n),
        grid_spec=pltpu.PrefetchScalarGridSpec(
            num_scalar_prefetch=1,
            grid=(steps,),
            in_specs=[shard_block(steps, k) for k in aheads],
            out_specs=[half_block(steps, OLD)] * (2 * n),
        ),
        out_shape=[half] * (2 * n),
        compiler_params=PARAMS,
        name=name,
    )(me, *([g] * n))


def sum_grad_kernel(own_a, own_b, ua, ub, da, db, out_ref):
    half = PEERS // 2
    for h, refs in enumerate(((own_a, ua, da), (own_b, ub, db))):
        for j in range(half):
            own, up, down = (ref[j].astype(F32) for ref in refs)
            out_ref[h * half + j] = (own + up + down).astype(BF16)


def sum_grad(*halves):
    return pl.pallas_call(
        sum_grad_kernel,
        out_shape=jax.ShapeDtypeStruct((PEERS, OLD, PR, PC), BF16),
        in_specs=[VMEM] * 6,
        out_specs=VMEM,
        compiler_params=PARAMS,
        name="sum_grad",
    )(*halves)


def adam_step(gradient, moment_one, moment_two, weight):
    moment_one = 0.9 * moment_one + 0.1 * gradient
    moment_two = 0.95 * moment_two + 0.05 * gradient * gradient
    scaled_one = moment_one * (1.0 / (1.0 - 0.9**50))
    scaled_two = moment_two * (1.0 / (1.0 - 0.95**50))
    update = scaled_one / (jnp.sqrt(scaled_two) + 1e-08)
    weight = weight - 0.05 * (update + 0.1 * weight)
    return (weight, moment_one, moment_two)


def update_kernel(table_ref, state_ref, grad_ref, weight_ref, moments_ref):
    def owner(d, _):
        for s in range(NEW):
            row = table_ref[d * NEW + s]
            has = row >= 0
            row = jnp.maximum(row, 0)
            gradient = grad_ref[row].astype(F32)
            m1 = state_ref[row, 0].astype(F32)
            m2 = state_ref[row, 1].astype(F32)
            w = state_ref[row, 2].astype(F32)
            w, m1, m2 = adam_step(gradient, m1, m2, w)
            weight_ref[d, s] = jnp.where(has, w, 0.0).astype(BF16)
            moments_ref[d, s, 0] = jnp.where(has, m1, 0.0).astype(BF16)
            moments_ref[d, s, 1] = jnp.where(has, m2, 0.0).astype(BF16)
        return 0

    lax.fori_loop(0, PEERS, owner, 0)


def update(table, state, grad):
    vmem = pl.BlockSpec(memory_space=pltpu.VMEM)
    return pl.pallas_call(
        update_kernel,
        out_shape=(
            jax.ShapeDtypeStruct((PEERS, NEW, PR, PC), BF16),
            jax.ShapeDtypeStruct((PEERS, NEW, 2, PR, PC), BF16),
        ),
        in_specs=[pl.BlockSpec(memory_space=pltpu.SMEM), vmem, vmem],
        out_specs=(vmem, vmem),
        compiler_params=PARAMS,
        name="update",
    )(table, state, grad)


def unpack_own_kernel(me_ref, w_ref, w_out, out_ref):
    del me_ref
    first = pl.program_id(0) * (PEERS // STEPS)
    for r in range(w_out.shape[1] // PR):
        for c in range(2):
            rows, lanes = slice(r * PR, (r + 1) * PR), slice(c * PC, (c + 1) * PC)
            piece = w_ref[first + 2 * r + c]
            w_out[:, rows, lanes] = piece.astype(F32)
            out_ref[:, rows, lanes] = piece


def unpack_own(me, w):
    rows = 128 // STEPS
    return pl.pallas_call(
        unpack_own_kernel,
        grid_spec=pltpu.PrefetchScalarGridSpec(
            num_scalar_prefetch=1,
            grid=(STEPS,),
            in_specs=[VMEM],
            out_specs=[
                pl.BlockSpec((NEW, rows, 512), lambda i, me: (0, i, 0)),
                pl.BlockSpec((NEW, rows, 512), lambda i, me: (0, i, me[0])),
            ],
        ),
        out_shape=(
            jax.ShapeDtypeStruct((NEW, 128, 512), F32),
            jax.ShapeDtypeStruct((NEW, 128, 2048), BF16),
        ),
        compiler_params=PARAMS,
        name="unpack_own",
    )(me, w)


def unpack_moments_kernel(m_ref, m1_out, m2_out):
    first = pl.program_id(0) * (PEERS // STEPS)
    for r in range(m1_out.shape[1] // PR):
        for c in range(2):
            rows, lanes = slice(r * PR, (r + 1) * PR), slice(c * PC, (c + 1) * PC)
            m1_out[:, rows, lanes] = m_ref[first + 2 * r + c, :, 0].astype(F32)
            m2_out[:, rows, lanes] = m_ref[first + 2 * r + c, :, 1].astype(F32)


def unpack_moments(m):
    rows = 128 // STEPS
    out = jax.ShapeDtypeStruct((NEW, 128, 512), F32)
    return pl.pallas_call(
        unpack_moments_kernel,
        grid=(STEPS,),
        out_shape=(out, out),
        in_specs=[VMEM],
        out_specs=[pl.BlockSpec((NEW, rows, 512), lambda i: (0, i, 0))] * 2,
        compiler_params=PARAMS,
        name="unpack_moments",
    )(m)


def unpack_block_kernel(me_ref, a_ref, b_ref, old_ref, out_ref):
    del me_ref, old_ref
    half = pl.program_id(0)

    def copy(ref):
        for r in range(out_ref.shape[1] // PR):
            for c in range(2):
                rows, lanes = slice(r * PR, (r + 1) * PR), slice(c * PC, (c + 1) * PC)
                out_ref[:, rows, lanes] = ref[2 * r + c]

    pl.when(half == 0)(lambda: copy(a_ref))
    pl.when(half == 1)(lambda: copy(b_ref))


def unpack_block(me, a, b, params, ahead):
    return pl.pallas_call(
        unpack_block_kernel,
        grid_spec=pltpu.PrefetchScalarGridSpec(
            num_scalar_prefetch=1,
            grid=(2,),
            in_specs=[VMEM, VMEM, pl.BlockSpec(memory_space=pl.ANY)],
            out_specs=pl.BlockSpec((NEW, 64, 512), lambda i, me: (0, i, (me[0] + ahead) % 4)),
        ),
        out_shape=jax.ShapeDtypeStruct((NEW, 128, 2048), BF16),
        input_output_aliases={3: 0},
        compiler_params=PARAMS,
        name="unpack_block",
    )(me, a, b, params)


UP = [(i, (i + 1) % 4) for i in range(4)]
DOWN = [(i, (i - 1) % 4) for i in range(4)]


def send_up(x):
    return lax.ppermute(x, "dp", UP)


def send_down(x):
    return lax.ppermute(x, "dp", DOWN)


def add(x, y):
    return (x.astype(F32) + y.astype(F32)).astype(BF16)


def exchange(values):
    return lax.all_to_all(values, "expert", split_axis=0, concat_axis=0, tiled=True)


def shards(grad_parts, first_moment, second_moment, master_weight, old_owner, new_owner):
    me = lax.axis_index("dp").astype(jnp.int32)[None]
    g = grad_parts[0].reshape(OLD, 2, 64, 2048)
    far_a, far_b = pack_halves(me, g, (2,), "pack_far")
    far_up, far_down = send_up(far_a), send_down(far_b)
    state = pack_state(first_moment, second_moment, master_weight)
    state, g = lax.optimization_barrier((state, g))
    state = exchange(state)
    up_a, up_b, down_a, down_b, own_a, own_b = pack_halves(me, g, (1, 3, 0), "pack_near")
    ub, da = send_up(up_b), send_down(down_a)
    ua, db = send_up(add(up_a, far_up)), send_down(add(down_b, far_down))
    state, ua, ub, da, db = lax.optimization_barrier((state, ua, ub, da, db))
    grad = exchange(sum_grad(own_a, own_b, ua, ub, da, db))
    table = route(old_owner, new_owner)
    weight, moments = update(
        table,
        state.reshape(PEERS * OLD, 3, PR, PC),
        grad.reshape(PEERS * OLD, PR, PC),
    )
    weight = exchange(weight)
    weight, moments = lax.optimization_barrier((weight, moments))
    wa, wb = weight[: PEERS // 2], weight[PEERS // 2 :]
    ua, da = send_up(wa), send_down(wa)
    ub, db = send_up(wb), send_down(wb)
    fa, fb = send_up(ua), send_down(db)
    moments = exchange(moments)
    new_master, params = unpack_own(me, weight)
    params = unpack_block(me, ua, ub, params, 3)
    params = unpack_block(me, da, db, params, 1)
    new_first, new_second = unpack_moments(moments)
    fa, fb, new_first = lax.optimization_barrier((fa, fb, new_first))
    new_params = unpack_block(me, fa, fb, params, 2)
    return (new_master, new_first, new_second, new_params)


def solution(mesh):
    placed = (
        P("dp", "expert", None, None),
        P("expert", None, "dp"),
        P("expert", None, "dp"),
        P("expert", None, "dp"),
        P(),
        P(),
    )
    return jax.shard_map(
        shards,
        mesh=mesh,
        in_specs=placed,
        out_specs=(
            P("expert", None, "dp"),
            P("expert", None, "dp"),
            P("expert", None, "dp"),
            P("expert", None, None),
        ),
        check_vma=False,
    )
```

```python
import functools

import jax
import jax.numpy as jnp
from jax import lax
from jax.experimental import pallas as pl
from jax.experimental.pallas import tpu as pltpu
from jax.sharding import PartitionSpec as P

BF16 = jnp.bfloat16
F32 = jnp.float32
PEERS = 32
OLD = 4
NEW = 6
PR, PC = 8, 256
STEPS = 2
PARAMS = pltpu.CompilerParams(vmem_limit_bytes=16 * 1024 * 1024)
VMEM = pl.BlockSpec(memory_space=pltpu.VMEM)


def route_kernel(old_ref, new_ref, state_ref, table_ref, staged_ref, old_count, new_count, sem):
    load = pltpu.make_async_copy(state_ref, staged_ref, sem)
    load.start()

    def clear_counts(i, _):
        old_count[i] = 0
        new_count[i] = 0
        return 0

    def clear_table(i, _):
        table_ref[i] = -1
        return 0

    lax.fori_loop(0, PEERS, clear_counts, 0)
    lax.fori_loop(0, PEERS * NEW, clear_table, 0)

    def place(t, _):
        o = old_ref[t]
        n = new_ref[t]
        a = old_count[o]
        b = new_count[n]
        table_ref[n * NEW + b] = o * OLD + a
        old_count[o] = a + 1
        new_count[n] = b + 1
        return 0

    lax.fori_loop(0, old_ref.shape[0], place, 0)
    load.wait()


def route(old_owner, new_owner, state):
    smem = pl.BlockSpec(memory_space=pltpu.SMEM)
    return pl.pallas_call(
        route_kernel,
        out_shape=(
            jax.ShapeDtypeStruct((PEERS * NEW,), jnp.int32),
            jax.ShapeDtypeStruct(state.shape, state.dtype),
        ),
        in_specs=[smem, smem, pl.BlockSpec(memory_space=pl.ANY)],
        out_specs=(smem, VMEM),
        scratch_shapes=[
            pltpu.SMEM((PEERS,), jnp.int32),
            pltpu.SMEM((PEERS,), jnp.int32),
            pltpu.SemaphoreType.DMA,
        ],
        compiler_params=PARAMS,
        name="route",
    )(old_owner, new_owner, state)


def pack_state_kernel(m1_ref, m2_ref, w_ref, out_ref):
    for k, ref in enumerate((m1_ref, m2_ref, w_ref)):
        for r in range(ref.shape[1] // PR):
            for c in range(2):
                piece = ref[:, r * PR : (r + 1) * PR, c * PC : (c + 1) * PC]
                out_ref[2 * r + c, :, k] = piece.astype(BF16)


def pack_state(m1, m2, w):
    rows = 128 // STEPS
    block = pl.BlockSpec((OLD, rows, 512), lambda i: (0, i, 0))
    return pl.pallas_call(
        pack_state_kernel,
        grid=(STEPS,),
        out_shape=jax.ShapeDtypeStruct((PEERS, OLD, 3, PR, PC), BF16),
        in_specs=[block] * 3,
        out_specs=pl.BlockSpec((PEERS // STEPS, OLD, 3, PR, PC), lambda i: (i, 0, 0, 0, 0)),
        name="pack_state",
    )(m1, m2, w)


def pack_halves_kernel(ahead, me_ref, *refs):
    del me_ref
    for g_ref, a_ref, b_ref in zip(refs[:ahead], refs[ahead::2], refs[ahead + 1 :: 2]):
        for r in range(g_ref.shape[2] // PR):
            for c in range(2):
                rows, lanes = slice(r * PR, (r + 1) * PR), slice(c * PC, (c + 1) * PC)
                a_ref[2 * r + c] = g_ref[:, 0, rows, lanes]
                b_ref[2 * r + c] = g_ref[:, 1, rows, lanes]


def shard_block(steps, ahead):
    return pl.BlockSpec((OLD, 2, 64 // steps, 512), lambda i, me: (0, 0, i, (me[0] + ahead) % 4))


def half_block(steps, slots):
    return pl.BlockSpec((PEERS // 2 // steps, slots, PR, PC), lambda i, me: (i, 0, 0, 0))


def pack_halves(me, g, aheads, name):
    steps = 2
    n = len(aheads)
    half = jax.ShapeDtypeStruct((PEERS // 2, OLD, PR, PC), BF16)
    return pl.pallas_call(
        functools.partial(pack_halves_kernel, n),
        grid_spec=pltpu.PrefetchScalarGridSpec(
            num_scalar_prefetch=1,
            grid=(steps,),
            in_specs=[shard_block(steps, k) for k in aheads],
            out_specs=[half_block(steps, OLD)] * (2 * n),
        ),
        out_shape=[half] * (2 * n),
        compiler_params=PARAMS,
        name=name,
    )(me, *([g] * n))


def sum_grad_kernel(own_a, own_b, ua, ub, da, db, out_ref):
    half = PEERS // 2
    for h, refs in enumerate(((own_a, ua, da), (own_b, ub, db))):
        for j in range(half):
            own, up, down = (ref[j].astype(F32) for ref in refs)
            out_ref[h * half + j] = (own + up + down).astype(BF16)


def sum_grad(*halves):
    return pl.pallas_call(
        sum_grad_kernel,
        out_shape=jax.ShapeDtypeStruct((PEERS, OLD, PR, PC), BF16),
        in_specs=[VMEM] * 6,
        out_specs=VMEM,
        compiler_params=PARAMS,
        name="sum_grad",
    )(*halves)


def adam_step(gradient, moment_one, moment_two, weight):
    moment_one = 0.9 * moment_one + 0.1 * gradient
    moment_two = 0.95 * moment_two + 0.05 * gradient * gradient
    scaled_one = moment_one * (1.0 / (1.0 - 0.9**50))
    scaled_two = moment_two * (1.0 / (1.0 - 0.95**50))
    update = scaled_one / (jnp.sqrt(scaled_two) + 1e-08)
    weight = weight - 0.05 * (update + 0.1 * weight)
    return (weight, moment_one, moment_two)


def update_kernel(table_ref, state_ref, grad_ref, weight_ref, moments_ref):
    def owner(d, _):
        for s in range(NEW):
            row = table_ref[d * NEW + s]
            has = row >= 0
            row = jnp.maximum(row, 0)
            gradient = grad_ref[row].astype(F32)
            m1 = state_ref[row, 0].astype(F32)
            m2 = state_ref[row, 1].astype(F32)
            w = state_ref[row, 2].astype(F32)
            w, m1, m2 = adam_step(gradient, m1, m2, w)
            weight_ref[d, s] = jnp.where(has, w, 0.0).astype(BF16)
            moments_ref[d, s, 0] = jnp.where(has, m1, 0.0).astype(BF16)
            moments_ref[d, s, 1] = jnp.where(has, m2, 0.0).astype(BF16)
        return 0

    lax.fori_loop(0, PEERS, owner, 0, unroll=2)


def update(table, state, grad):
    vmem = pl.BlockSpec(memory_space=pltpu.VMEM)
    return pl.pallas_call(
        update_kernel,
        out_shape=(
            jax.ShapeDtypeStruct((PEERS, NEW, PR, PC), BF16),
            jax.ShapeDtypeStruct((PEERS, NEW, 2, PR, PC), BF16),
        ),
        in_specs=[pl.BlockSpec(memory_space=pltpu.SMEM), vmem, vmem],
        out_specs=(vmem, vmem),
        compiler_params=PARAMS,
        name="update",
    )(table, state, grad)


def unpack_own_kernel(me_ref, w_ref, w_out, out_ref):
    del me_ref
    first = pl.program_id(0) * (PEERS // STEPS)
    for r in range(w_out.shape[1] // PR):
        for c in range(2):
            rows, lanes = slice(r * PR, (r + 1) * PR), slice(c * PC, (c + 1) * PC)
            piece = w_ref[first + 2 * r + c]
            w_out[:, rows, lanes] = piece.astype(F32)
            out_ref[:, rows, lanes] = piece


def unpack_own(me, w):
    rows = 128 // STEPS
    return pl.pallas_call(
        unpack_own_kernel,
        grid_spec=pltpu.PrefetchScalarGridSpec(
            num_scalar_prefetch=1,
            grid=(STEPS,),
            in_specs=[VMEM],
            out_specs=[
                pl.BlockSpec((NEW, rows, 512), lambda i, me: (0, i, 0)),
                pl.BlockSpec((NEW, rows, 512), lambda i, me: (0, i, me[0])),
            ],
        ),
        out_shape=(
            jax.ShapeDtypeStruct((NEW, 128, 512), F32),
            jax.ShapeDtypeStruct((NEW, 128, 2048), BF16),
        ),
        compiler_params=PARAMS,
        name="unpack_own",
    )(me, w)


def unpack_moments_kernel(m_ref, m1_out, m2_out):
    first = pl.program_id(0) * (PEERS // STEPS)
    for r in range(m1_out.shape[1] // PR):
        for c in range(2):
            rows, lanes = slice(r * PR, (r + 1) * PR), slice(c * PC, (c + 1) * PC)
            m1_out[:, rows, lanes] = m_ref[first + 2 * r + c, :, 0].astype(F32)
            m2_out[:, rows, lanes] = m_ref[first + 2 * r + c, :, 1].astype(F32)


def unpack_moments(m):
    rows = 128 // STEPS
    out = jax.ShapeDtypeStruct((NEW, 128, 512), F32)
    return pl.pallas_call(
        unpack_moments_kernel,
        grid=(STEPS,),
        out_shape=(out, out),
        in_specs=[VMEM],
        out_specs=[pl.BlockSpec((NEW, rows, 512), lambda i: (0, i, 0))] * 2,
        compiler_params=PARAMS,
        name="unpack_moments",
    )(m)


def unpack_block_kernel(me_ref, a_ref, b_ref, old_ref, out_ref):
    del me_ref, old_ref
    half = pl.program_id(0)

    def copy(ref):
        for r in range(out_ref.shape[1] // PR):
            for c in range(2):
                rows, lanes = slice(r * PR, (r + 1) * PR), slice(c * PC, (c + 1) * PC)
                out_ref[:, rows, lanes] = ref[2 * r + c]

    pl.when(half == 0)(lambda: copy(a_ref))
    pl.when(half == 1)(lambda: copy(b_ref))


def unpack_block(me, a, b, params, ahead):
    return pl.pallas_call(
        unpack_block_kernel,
        grid_spec=pltpu.PrefetchScalarGridSpec(
            num_scalar_prefetch=1,
            grid=(2,),
            in_specs=[VMEM, VMEM, pl.BlockSpec(memory_space=pl.ANY)],
            out_specs=pl.BlockSpec((NEW, 64, 512), lambda i, me: (0, i, (me[0] + ahead) % 4)),
        ),
        out_shape=jax.ShapeDtypeStruct((NEW, 128, 2048), BF16),
        input_output_aliases={3: 0},
        compiler_params=PARAMS,
        name="unpack_block",
    )(me, a, b, params)


UP = [(i, (i + 1) % 4) for i in range(4)]
DOWN = [(i, (i - 1) % 4) for i in range(4)]


def send_up(x):
    return lax.ppermute(x, "dp", UP)


def send_down(x):
    return lax.ppermute(x, "dp", DOWN)


def add(x, y):
    return (x.astype(F32) + y.astype(F32)).astype(BF16)


def exchange(values):
    return lax.all_to_all(values, "expert", split_axis=0, concat_axis=0, tiled=True)


def shards(grad_parts, first_moment, second_moment, master_weight, old_owner, new_owner):
    me = lax.axis_index("dp").astype(jnp.int32)[None]
    g = grad_parts[0].reshape(OLD, 2, 64, 2048)
    far_a, far_b = pack_halves(me, g, (2,), "pack_far")
    far_up, far_down = send_up(far_a), send_down(far_b)
    state = pack_state(first_moment, second_moment, master_weight)
    state, g = lax.optimization_barrier((state, g))
    state = exchange(state)
    up_a, up_b, down_a, down_b, own_a, own_b = pack_halves(me, g, (1, 3, 0), "pack_near")
    ub, da = send_up(up_b), send_down(down_a)
    ua, db = send_up(add(up_a, far_up)), send_down(add(down_b, far_down))
    state, ua, ub, da, db = lax.optimization_barrier((state, ua, ub, da, db))
    grad = exchange(sum_grad(own_a, own_b, ua, ub, da, db))
    table, state = route(old_owner, new_owner, state.reshape(PEERS * OLD, 3, PR, PC))
    weight, moments = update(
        table,
        state,
        grad.reshape(PEERS * OLD, PR, PC),
    )
    weight = exchange(weight)
    weight, moments = lax.optimization_barrier((weight, moments))
    wa, wb = weight[: PEERS // 2], weight[PEERS // 2 :]
    ua, da = send_up(wa), send_down(wa)
    ub, db = send_up(wb), send_down(wb)
    fa, fb = send_up(ua), send_down(db)
    moments = exchange(moments)
    new_master, params = unpack_own(me, weight)
    params = unpack_block(me, ua, ub, params, 3)
    params = unpack_block(me, da, db, params, 1)
    new_first, new_second = unpack_moments(moments)
    fa, fb, new_first = lax.optimization_barrier((fa, fb, new_first))
    new_params = unpack_block(me, fa, fb, params, 2)
    return (new_master, new_first, new_second, new_params)


def solution(mesh):
    placed = (
        P("dp", "expert", None, None),
        P("expert", None, "dp"),
        P("expert", None, "dp"),
        P("expert", None, "dp"),
        P(),
        P(),
    )
    return jax.shard_map(
        shards,
        mesh=mesh,
        in_specs=placed,
        out_specs=(
            P("expert", None, "dp"),
            P("expert", None, "dp"),
            P("expert", None, "dp"),
            P("expert", None, None),
        ),
        check_vma=False,
    )
```

```python
import functools

import jax
import jax.numpy as jnp
from jax import lax
from jax.experimental import pallas as pl
from jax.experimental.pallas import tpu as pltpu
from jax.sharding import PartitionSpec as P

BF16 = jnp.bfloat16
F32 = jnp.float32
PEERS = 32
OLD = 4
NEW = 6
PR, PC = 8, 256
STEPS = 2
PARAMS = pltpu.CompilerParams(vmem_limit_bytes=16 * 1024 * 1024)
VMEM = pl.BlockSpec(memory_space=pltpu.VMEM)


def route_kernel(old_ref, new_ref, state_ref, table_ref, staged_ref, old_count, new_count, sem):
    load = pltpu.make_async_copy(state_ref, staged_ref, sem)
    load.start()

    def clear_counts(i, _):
        old_count[i] = 0
        new_count[i] = 0
        return 0

    def clear_table(i, _):
        table_ref[i] = -1
        return 0

    lax.fori_loop(0, PEERS, clear_counts, 0)
    lax.fori_loop(0, PEERS * NEW, clear_table, 0)

    def place(t, _):
        o = old_ref[t]
        n = new_ref[t]
        a = old_count[o]
        b = new_count[n]
        table_ref[n * NEW + b] = o * OLD + a
        old_count[o] = a + 1
        new_count[n] = b + 1
        return 0

    lax.fori_loop(0, old_ref.shape[0], place, 0)
    load.wait()


def route(old_owner, new_owner, state):
    smem = pl.BlockSpec(memory_space=pltpu.SMEM)
    return pl.pallas_call(
        route_kernel,
        out_shape=(
            jax.ShapeDtypeStruct((PEERS * NEW,), jnp.int32),
            jax.ShapeDtypeStruct(state.shape, state.dtype),
        ),
        in_specs=[smem, smem, pl.BlockSpec(memory_space=pl.ANY)],
        out_specs=(smem, VMEM),
        scratch_shapes=[
            pltpu.SMEM((PEERS,), jnp.int32),
            pltpu.SMEM((PEERS,), jnp.int32),
            pltpu.SemaphoreType.DMA,
        ],
        compiler_params=PARAMS,
        name="route",
    )(old_owner, new_owner, state)


def pack_state_kernel(m1_ref, m2_ref, w_ref, out_ref):
    for k, ref in enumerate((m1_ref, m2_ref, w_ref)):
        for r in range(ref.shape[1] // PR):
            for c in range(2):
                piece = ref[:, r * PR : (r + 1) * PR, c * PC : (c + 1) * PC]
                out_ref[2 * r + c, :, k] = piece.astype(BF16)


def pack_state(m1, m2, w):
    rows = 128 // STEPS
    block = pl.BlockSpec((OLD, rows, 512), lambda i: (0, i, 0))
    return pl.pallas_call(
        pack_state_kernel,
        grid=(STEPS,),
        out_shape=jax.ShapeDtypeStruct((PEERS, OLD, 3, PR, PC), BF16),
        in_specs=[block] * 3,
        out_specs=pl.BlockSpec((PEERS // STEPS, OLD, 3, PR, PC), lambda i: (i, 0, 0, 0, 0)),
        name="pack_state",
    )(m1, m2, w)


def pack_halves_kernel(ahead, me_ref, *refs):
    del me_ref
    for g_ref, a_ref, b_ref in zip(refs[:ahead], refs[ahead::2], refs[ahead + 1 :: 2]):
        for r in range(g_ref.shape[2] // PR):
            for c in range(2):
                rows, lanes = slice(r * PR, (r + 1) * PR), slice(c * PC, (c + 1) * PC)
                a_ref[2 * r + c] = g_ref[:, 0, rows, lanes]
                b_ref[2 * r + c] = g_ref[:, 1, rows, lanes]


def shard_block(steps, ahead):
    return pl.BlockSpec((OLD, 2, 64 // steps, 512), lambda i, me: (0, 0, i, (me[0] + ahead) % 4))


def half_block(steps, slots):
    return pl.BlockSpec((PEERS // 2 // steps, slots, PR, PC), lambda i, me: (i, 0, 0, 0))


def pack_halves(me, g, aheads, name):
    steps = 2
    n = len(aheads)
    half = jax.ShapeDtypeStruct((PEERS // 2, OLD, PR, PC), BF16)
    return pl.pallas_call(
        functools.partial(pack_halves_kernel, n),
        grid_spec=pltpu.PrefetchScalarGridSpec(
            num_scalar_prefetch=1,
            grid=(steps,),
            in_specs=[shard_block(steps, k) for k in aheads],
            out_specs=[half_block(steps, OLD)] * (2 * n),
        ),
        out_shape=[half] * (2 * n),
        compiler_params=PARAMS,
        name=name,
    )(me, *([g] * n))


def sum_grad_kernel(own_a, own_b, ua, ub, da, db, out_ref):
    half = PEERS // 2
    for h, refs in enumerate(((own_a, ua, da), (own_b, ub, db))):
        for j in range(half):
            own, up, down = (ref[j].astype(F32) for ref in refs)
            out_ref[h * half + j] = (own + up + down).astype(BF16)


def sum_grad(*halves):
    return pl.pallas_call(
        sum_grad_kernel,
        out_shape=jax.ShapeDtypeStruct((PEERS, OLD, PR, PC), BF16),
        in_specs=[VMEM] * 6,
        out_specs=VMEM,
        compiler_params=PARAMS,
        name="sum_grad",
    )(*halves)


def adam_step(gradient, moment_one, moment_two, weight):
    moment_one = 0.9 * moment_one + 0.1 * gradient
    moment_two = 0.95 * moment_two + 0.05 * gradient * gradient
    scaled_one = moment_one * (1.0 / (1.0 - 0.9**50))
    scaled_two = moment_two * (1.0 / (1.0 - 0.95**50))
    update = scaled_one / (jnp.sqrt(scaled_two) + 1e-08)
    weight = weight - 0.05 * (update + 0.1 * weight)
    return (weight, moment_one, moment_two)


def update_kernel(table_ref, state_ref, grad_ref, weight_ref, moments_ref):
    def owner(d, _):
        for s in range(NEW):
            row = table_ref[d * NEW + s]
            has = row >= 0
            row = jnp.maximum(row, 0)
            gradient = grad_ref[row].astype(F32)
            m1 = state_ref[row, 0].astype(F32)
            m2 = state_ref[row, 1].astype(F32)
            w = state_ref[row, 2].astype(F32)
            w, m1, m2 = adam_step(gradient, m1, m2, w)
            weight_ref[d, s] = jnp.where(has, w, 0.0).astype(BF16)
            moments_ref[d, s, 0] = jnp.where(has, m1, 0.0).astype(BF16)
            moments_ref[d, s, 1] = jnp.where(has, m2, 0.0).astype(BF16)
        return 0

    lax.fori_loop(0, PEERS, owner, 0, unroll=2)


def update(table, state, grad):
    vmem = pl.BlockSpec(memory_space=pltpu.VMEM)
    return pl.pallas_call(
        update_kernel,
        out_shape=(
            jax.ShapeDtypeStruct((PEERS, NEW, PR, PC), BF16),
            jax.ShapeDtypeStruct((PEERS, NEW, 2, PR, PC), BF16),
        ),
        in_specs=[pl.BlockSpec(memory_space=pltpu.SMEM), vmem, vmem],
        out_specs=(vmem, vmem),
        compiler_params=PARAMS,
        name="update",
    )(table, state, grad)


def unpack_own_kernel(me_ref, w_ref, w_out, out_ref):
    del me_ref
    first = pl.program_id(0) * (PEERS // STEPS)
    for r in range(w_out.shape[1] // PR):
        for c in range(2):
            rows, lanes = slice(r * PR, (r + 1) * PR), slice(c * PC, (c + 1) * PC)
            piece = w_ref[first + 2 * r + c]
            w_out[:, rows, lanes] = piece.astype(F32)
            out_ref[:, rows, lanes] = piece


def unpack_own(me, w):
    rows = 128 // STEPS
    return pl.pallas_call(
        unpack_own_kernel,
        grid_spec=pltpu.PrefetchScalarGridSpec(
            num_scalar_prefetch=1,
            grid=(STEPS,),
            in_specs=[VMEM],
            out_specs=[
                pl.BlockSpec((NEW, rows, 512), lambda i, me: (0, i, 0)),
                pl.BlockSpec((NEW, rows, 512), lambda i, me: (0, i, me[0])),
            ],
        ),
        out_shape=(
            jax.ShapeDtypeStruct((NEW, 128, 512), F32),
            jax.ShapeDtypeStruct((NEW, 128, 2048), BF16),
        ),
        compiler_params=PARAMS,
        name="unpack_own",
    )(me, w)


def unpack_moments_kernel(m_ref, m1_out, m2_out):
    first = pl.program_id(0) * (PEERS // STEPS)
    for r in range(m1_out.shape[1] // PR):
        for c in range(2):
            rows, lanes = slice(r * PR, (r + 1) * PR), slice(c * PC, (c + 1) * PC)
            m1_out[:, rows, lanes] = m_ref[first + 2 * r + c, :, 0].astype(F32)
            m2_out[:, rows, lanes] = m_ref[first + 2 * r + c, :, 1].astype(F32)


def unpack_moments(m):
    rows = 128 // STEPS
    out = jax.ShapeDtypeStruct((NEW, 128, 512), F32)
    return pl.pallas_call(
        unpack_moments_kernel,
        grid=(STEPS,),
        out_shape=(out, out),
        in_specs=[VMEM],
        out_specs=[pl.BlockSpec((NEW, rows, 512), lambda i: (0, i, 0))] * 2,
        compiler_params=PARAMS,
        name="unpack_moments",
    )(m)


def unpack_block_kernel(me_ref, a_ref, b_ref, old_ref, out_ref):
    del me_ref, old_ref
    half = pl.program_id(0)

    def copy(ref):
        for r in range(out_ref.shape[1] // PR):
            for c in range(2):
                rows, lanes = slice(r * PR, (r + 1) * PR), slice(c * PC, (c + 1) * PC)
                out_ref[:, rows, lanes] = ref[2 * r + c]

    pl.when(half == 0)(lambda: copy(a_ref))
    pl.when(half == 1)(lambda: copy(b_ref))


def unpack_block(me, a, b, params, ahead):
    return pl.pallas_call(
        unpack_block_kernel,
        grid_spec=pltpu.PrefetchScalarGridSpec(
            num_scalar_prefetch=1,
            grid=(2,),
            in_specs=[VMEM, VMEM, pl.BlockSpec(memory_space=pl.ANY)],
            out_specs=pl.BlockSpec((NEW, 64, 512), lambda i, me: (0, i, (me[0] + ahead) % 4)),
        ),
        out_shape=jax.ShapeDtypeStruct((NEW, 128, 2048), BF16),
        input_output_aliases={3: 0},
        compiler_params=PARAMS,
        name="unpack_block",
    )(me, a, b, params)


UP = [(i, (i + 1) % 4) for i in range(4)]
DOWN = [(i, (i - 1) % 4) for i in range(4)]


def send_up(x):
    return lax.ppermute(x, "dp", UP)


def send_down(x):
    return lax.ppermute(x, "dp", DOWN)


def add(x, y):
    return (x.astype(F32) + y.astype(F32)).astype(BF16)


def exchange(values):
    return lax.all_to_all(values, "expert", split_axis=0, concat_axis=0, tiled=True)


def shards(grad_parts, first_moment, second_moment, master_weight, old_owner, new_owner):
    me = lax.axis_index("dp").astype(jnp.int32)[None]
    g = grad_parts[0].reshape(OLD, 2, 64, 2048)
    far_a, far_b = pack_halves(me, g, (2,), "pack_far")
    far_up, far_down = send_up(far_a), send_down(far_b)
    state = pack_state(first_moment, second_moment, master_weight)
    state, g = lax.optimization_barrier((state, g))
    state = exchange(state)
    up_a, up_b, down_a, down_b, own_a, own_b = pack_halves(me, g, (1, 3, 0), "pack_near")
    ub, da = send_up(up_b), send_down(down_a)
    ua, db = send_up(add(up_a, far_up)), send_down(add(down_b, far_down))
    state, ua, ub, da, db = lax.optimization_barrier((state, ua, ub, da, db))
    grad = exchange(sum_grad(own_a, own_b, ua, ub, da, db))
    table, state = route(old_owner, new_owner, state.reshape(PEERS * OLD, 3, PR, PC))
    weight, moments = update(
        table,
        state,
        grad.reshape(PEERS * OLD, PR, PC),
    )
    weight = exchange(weight)
    weight, moments = lax.optimization_barrier((weight, moments))
    wa, wb = weight[: PEERS // 2], weight[PEERS // 2 :]
    ua, da = send_up(wa), send_down(wa)
    ub, db = send_up(wb), send_down(wb)
    moments = exchange(moments)
    new_master, params = unpack_own(me, weight)
    far_up, far_down, params = lax.optimization_barrier((ua, db, params))
    fa, fb = send_up(far_up), send_down(far_down)
    params = unpack_block(me, ua, ub, params, 3)
    params = unpack_block(me, da, db, params, 1)
    new_first, new_second = unpack_moments(moments)
    fa, fb, new_first = lax.optimization_barrier((fa, fb, new_first))
    new_params = unpack_block(me, fa, fb, params, 2)
    return (new_master, new_first, new_second, new_params)


def solution(mesh):
    placed = (
        P("dp", "expert", None, None),
        P("expert", None, "dp"),
        P("expert", None, "dp"),
        P("expert", None, "dp"),
        P(),
        P(),
    )
    return jax.shard_map(
        shards,
        mesh=mesh,
        in_specs=placed,
        out_specs=(
            P("expert", None, "dp"),
            P("expert", None, "dp"),
            P("expert", None, "dp"),
            P("expert", None, None),
        ),
        check_vma=False,
    )
```

```python
import functools

import jax
import jax.numpy as jnp
from jax import lax
from jax.experimental import pallas as pl
from jax.experimental.pallas import tpu as pltpu
from jax.sharding import PartitionSpec as P

BF16 = jnp.bfloat16
F32 = jnp.float32
PEERS = 32
OLD = 4
NEW = 6
PR, PC = 8, 256
STEPS = 2
PARAMS = pltpu.CompilerParams(vmem_limit_bytes=16 * 1024 * 1024)
VMEM = pl.BlockSpec(memory_space=pltpu.VMEM)


def route_kernel(old_ref, new_ref, state_ref, table_ref, staged_ref, old_count, new_count, sem):
    load = pltpu.make_async_copy(state_ref, staged_ref, sem)
    load.start()

    def clear_counts(i, _):
        old_count[i] = 0
        new_count[i] = 0
        return 0

    def clear_table(i, _):
        table_ref[i] = -1
        return 0

    lax.fori_loop(0, PEERS, clear_counts, 0)
    lax.fori_loop(0, PEERS * NEW, clear_table, 0)

    def place(t, _):
        o = old_ref[t]
        n = new_ref[t]
        a = old_count[o]
        b = new_count[n]
        table_ref[n * NEW + b] = o * OLD + a
        old_count[o] = a + 1
        new_count[n] = b + 1
        return 0

    lax.fori_loop(0, old_ref.shape[0], place, 0)
    load.wait()


def route(old_owner, new_owner, state):
    smem = pl.BlockSpec(memory_space=pltpu.SMEM)
    return pl.pallas_call(
        route_kernel,
        out_shape=(
            jax.ShapeDtypeStruct((PEERS * NEW,), jnp.int32),
            jax.ShapeDtypeStruct(state.shape, state.dtype),
        ),
        in_specs=[smem, smem, pl.BlockSpec(memory_space=pl.ANY)],
        out_specs=(smem, VMEM),
        scratch_shapes=[
            pltpu.SMEM((PEERS,), jnp.int32),
            pltpu.SMEM((PEERS,), jnp.int32),
            pltpu.SemaphoreType.DMA,
        ],
        compiler_params=PARAMS,
        name="route",
    )(old_owner, new_owner, state)


def pack_state_kernel(m1_ref, m2_ref, w_ref, out_ref):
    for k, ref in enumerate((m1_ref, m2_ref, w_ref)):
        for r in range(ref.shape[1] // PR):
            for c in range(2):
                piece = ref[:, r * PR : (r + 1) * PR, c * PC : (c + 1) * PC]
                out_ref[2 * r + c, :, k] = piece.astype(BF16)


def pack_state(m1, m2, w):
    rows = 128 // STEPS
    block = pl.BlockSpec((OLD, rows, 512), lambda i: (0, i, 0))
    return pl.pallas_call(
        pack_state_kernel,
        grid=(STEPS,),
        out_shape=jax.ShapeDtypeStruct((PEERS, OLD, 3, PR, PC), BF16),
        in_specs=[block] * 3,
        out_specs=pl.BlockSpec((PEERS // STEPS, OLD, 3, PR, PC), lambda i: (i, 0, 0, 0, 0)),
        name="pack_state",
    )(m1, m2, w)


def pack_halves_kernel(ahead, me_ref, *refs):
    del me_ref
    for g_ref, a_ref, b_ref in zip(refs[:ahead], refs[ahead::2], refs[ahead + 1 :: 2]):
        for r in range(g_ref.shape[2] // PR):
            for c in range(2):
                rows, lanes = slice(r * PR, (r + 1) * PR), slice(c * PC, (c + 1) * PC)
                a_ref[2 * r + c] = g_ref[:, 0, rows, lanes]
                b_ref[2 * r + c] = g_ref[:, 1, rows, lanes]


def shard_block(steps, ahead):
    return pl.BlockSpec((OLD, 2, 64 // steps, 512), lambda i, me: (0, 0, i, (me[0] + ahead) % 4))


def half_block(steps, slots):
    return pl.BlockSpec((PEERS // 2 // steps, slots, PR, PC), lambda i, me: (i, 0, 0, 0))


def pack_halves(me, g, aheads, name):
    steps = 2
    n = len(aheads)
    half = jax.ShapeDtypeStruct((PEERS // 2, OLD, PR, PC), BF16)
    return pl.pallas_call(
        functools.partial(pack_halves_kernel, n),
        grid_spec=pltpu.PrefetchScalarGridSpec(
            num_scalar_prefetch=1,
            grid=(steps,),
            in_specs=[shard_block(steps, k) for k in aheads],
            out_specs=[half_block(steps, OLD)] * (2 * n),
        ),
        out_shape=[half] * (2 * n),
        compiler_params=PARAMS,
        name=name,
    )(me, *([g] * n))


def sum_grad_kernel(own_a, own_b, ua, ub, da, db, out_ref):
    half = PEERS // 2
    for h, refs in enumerate(((own_a, ua, da), (own_b, ub, db))):
        for j in range(half):
            own, up, down = (ref[j].astype(F32) for ref in refs)
            out_ref[PEERS - 1 - (h * half + j)] = (own + up + down).astype(BF16)


def sum_grad(*halves):
    return pl.pallas_call(
        sum_grad_kernel,
        out_shape=jax.ShapeDtypeStruct((PEERS, OLD, PR, PC), BF16),
        in_specs=[VMEM] * 6,
        out_specs=VMEM,
        compiler_params=PARAMS,
        name="sum_grad",
    )(*halves)


def adam_step(gradient, moment_one, moment_two, weight):
    moment_one = 0.9 * moment_one + 0.1 * gradient
    moment_two = 0.95 * moment_two + 0.05 * gradient * gradient
    scaled_one = moment_one * (1.0 / (1.0 - 0.9**50))
    scaled_two = moment_two * (1.0 / (1.0 - 0.95**50))
    update = scaled_one / (jnp.sqrt(scaled_two) + 1e-08)
    weight = weight - 0.05 * (update + 0.1 * weight)
    return (weight, moment_one, moment_two)


def update_kernel(table_ref, state_ref, grad_ref, weight_ref, moments_ref):
    def owner(d, _):
        for s in range(NEW):
            row = table_ref[d * NEW + s]
            has = row >= 0
            row = jnp.maximum(row, 0)
            gradient = grad_ref[row ^ ((PEERS - 1) * OLD)].astype(F32)
            m1 = state_ref[row, 0].astype(F32)
            m2 = state_ref[row, 1].astype(F32)
            w = state_ref[row, 2].astype(F32)
            w, m1, m2 = adam_step(gradient, m1, m2, w)
            weight_ref[PEERS - 1 - d, s] = jnp.where(has, w, 0.0).astype(BF16)
            moments_ref[d, s, 0] = jnp.where(has, m1, 0.0).astype(BF16)
            moments_ref[d, s, 1] = jnp.where(has, m2, 0.0).astype(BF16)
        return 0

    lax.fori_loop(0, PEERS, owner, 0, unroll=2)


def update(table, state, grad):
    vmem = pl.BlockSpec(memory_space=pltpu.VMEM)
    return pl.pallas_call(
        update_kernel,
        out_shape=(
            jax.ShapeDtypeStruct((PEERS, NEW, PR, PC), BF16),
            jax.ShapeDtypeStruct((PEERS, NEW, 2, PR, PC), BF16),
        ),
        in_specs=[pl.BlockSpec(memory_space=pltpu.SMEM), vmem, vmem],
        out_specs=(vmem, vmem),
        compiler_params=PARAMS,
        name="update",
    )(table, state, grad)


def unpack_own_kernel(me_ref, w_ref, w_out, out_ref):
    del me_ref
    first = pl.program_id(0) * (PEERS // STEPS)
    for r in range(w_out.shape[1] // PR):
        for c in range(2):
            rows, lanes = slice(r * PR, (r + 1) * PR), slice(c * PC, (c + 1) * PC)
            piece = w_ref[PEERS - 1 - (first + 2 * r + c)]
            w_out[:, rows, lanes] = piece.astype(F32)
            out_ref[:, rows, lanes] = piece


def unpack_own(me, w):
    rows = 128 // STEPS
    return pl.pallas_call(
        unpack_own_kernel,
        grid_spec=pltpu.PrefetchScalarGridSpec(
            num_scalar_prefetch=1,
            grid=(STEPS,),
            in_specs=[VMEM],
            out_specs=[
                pl.BlockSpec((NEW, rows, 512), lambda i, me: (0, i, 0)),
                pl.BlockSpec((NEW, rows, 512), lambda i, me: (0, i, me[0])),
            ],
        ),
        out_shape=(
            jax.ShapeDtypeStruct((NEW, 128, 512), F32),
            jax.ShapeDtypeStruct((NEW, 128, 2048), BF16),
        ),
        compiler_params=PARAMS,
        name="unpack_own",
    )(me, w)


def unpack_moments_kernel(m_ref, m1_out, m2_out):
    first = pl.program_id(0) * (PEERS // STEPS)
    for r in range(m1_out.shape[1] // PR):
        for c in range(2):
            rows, lanes = slice(r * PR, (r + 1) * PR), slice(c * PC, (c + 1) * PC)
            m1_out[:, rows, lanes] = m_ref[first + 2 * r + c, :, 0].astype(F32)
            m2_out[:, rows, lanes] = m_ref[first + 2 * r + c, :, 1].astype(F32)


def unpack_moments(m):
    rows = 128 // STEPS
    out = jax.ShapeDtypeStruct((NEW, 128, 512), F32)
    return pl.pallas_call(
        unpack_moments_kernel,
        grid=(STEPS,),
        out_shape=(out, out),
        in_specs=[VMEM],
        out_specs=[pl.BlockSpec((NEW, rows, 512), lambda i: (0, i, 0))] * 2,
        compiler_params=PARAMS,
        name="unpack_moments",
    )(m)


def unpack_block_kernel(me_ref, a_ref, b_ref, old_ref, out_ref):
    del me_ref, old_ref
    half = pl.program_id(0)

    def copy(ref):
        for r in range(out_ref.shape[1] // PR):
            for c in range(2):
                rows, lanes = slice(r * PR, (r + 1) * PR), slice(c * PC, (c + 1) * PC)
                out_ref[:, rows, lanes] = ref[PEERS // 2 - 1 - (2 * r + c)]

    pl.when(half == 0)(lambda: copy(a_ref))
    pl.when(half == 1)(lambda: copy(b_ref))


def unpack_block(me, a, b, params, ahead):
    return pl.pallas_call(
        unpack_block_kernel,
        grid_spec=pltpu.PrefetchScalarGridSpec(
            num_scalar_prefetch=1,
            grid=(2,),
            in_specs=[VMEM, VMEM, pl.BlockSpec(memory_space=pl.ANY)],
            out_specs=pl.BlockSpec((NEW, 64, 512), lambda i, me: (0, i, (me[0] + ahead) % 4)),
        ),
        out_shape=jax.ShapeDtypeStruct((NEW, 128, 2048), BF16),
        input_output_aliases={3: 0},
        compiler_params=PARAMS,
        name="unpack_block",
    )(me, a, b, params)


UP = [(i, (i + 1) % 4) for i in range(4)]
DOWN = [(i, (i - 1) % 4) for i in range(4)]


def send_up(x):
    return lax.ppermute(x, "dp", UP)


def send_down(x):
    return lax.ppermute(x, "dp", DOWN)


def add(x, y):
    return (x.astype(F32) + y.astype(F32)).astype(BF16)


def exchange(values):
    return lax.all_to_all(values, "expert", split_axis=0, concat_axis=0, tiled=True)


def exchange_backward(values):
    order = [list(range(PEERS - 1, -1, -1))]
    return lax.all_to_all(values, "expert", split_axis=0, concat_axis=0, tiled=True, axis_index_groups=order)


def shards(grad_parts, first_moment, second_moment, master_weight, old_owner, new_owner):
    me = lax.axis_index("dp").astype(jnp.int32)[None]
    g = grad_parts[0].reshape(OLD, 2, 64, 2048)
    far_a, far_b = pack_halves(me, g, (2,), "pack_far")
    far_up, far_down = send_up(far_a), send_down(far_b)
    state = pack_state(first_moment, second_moment, master_weight)
    state, g = lax.optimization_barrier((state, g))
    state = exchange(state)
    up_a, up_b, down_a, down_b, own_a, own_b = pack_halves(me, g, (1, 3, 0), "pack_near")
    ub, da = send_up(up_b), send_down(down_a)
    ua, db = send_up(add(up_a, far_up)), send_down(add(down_b, far_down))
    state, ua, ub, da, db = lax.optimization_barrier((state, ua, ub, da, db))
    grad = exchange_backward(sum_grad(own_a, own_b, ua, ub, da, db))
    table, state = route(old_owner, new_owner, state.reshape(PEERS * OLD, 3, PR, PC))
    weight, moments = update(
        table,
        state,
        grad.reshape(PEERS * OLD, PR, PC),
    )
    weight = exchange_backward(weight)
    weight, moments = lax.optimization_barrier((weight, moments))
    wb, wa = weight[: PEERS // 2], weight[PEERS // 2 :]
    ua, da = send_up(wa), send_down(wa)
    ub, db = send_up(wb), send_down(wb)
    moments = exchange(moments)
    new_master, params = unpack_own(me, weight)
    far_up, far_down, params = lax.optimization_barrier((ua, db, params))
    fa, fb = send_up(far_up), send_down(far_down)
    params = unpack_block(me, ua, ub, params, 3)
    params = unpack_block(me, da, db, params, 1)
    new_first, new_second = unpack_moments(moments)
    fa, fb, new_first = lax.optimization_barrier((fa, fb, new_first))
    new_params = unpack_block(me, fa, fb, params, 2)
    return (new_master, new_first, new_second, new_params)


def solution(mesh):
    placed = (
        P("dp", "expert", None, None),
        P("expert", None, "dp"),
        P("expert", None, "dp"),
        P("expert", None, "dp"),
        P(),
        P(),
    )
    return jax.shard_map(
        shards,
        mesh=mesh,
        in_specs=placed,
        out_specs=(
            P("expert", None, "dp"),
            P("expert", None, "dp"),
            P("expert", None, "dp"),
            P("expert", None, None),
        ),
        check_vma=False,
    )
```
